32 devices in a mesh: row: 4 (over z), col: 8 (over y, x, core).
Axes of the slice: x: 2, y: 2, z: 4, core: 2. Of those that a mesh axis runs over, the one named last changes fastest.
Arguments:
- x_blocks: bfloat16 [1024, 1024, 128], P('row', 'col'), may hold values from -0.0625 to 0.0625
- block_ids: int32 [1024, 8], P('row', 'col'), may hold values from 0 to 511, as said below
- margins: float32 [16384], P('row'), may hold values from -6 to 6
- deleted: int32 [2048], P('row'), may hold values from 0 to 16383, as said below
- grads: float32 [16384, 128], P('col'), may hold values from -6 to 6
Outputs:
- solution: float32 [16384, 128], P('col')
- residual: float32 [16384, 128], P('col')
The draws below stay inside these ranges and needn't reach their ends.
Inputs may be any that keep to these rules, and one draw needn't show every extreme that they name: `block_ids`: each device's 256 entries are distinct and rise; each device lists the first and the last block of its grid. `deleted`: the 512 entries of row shard r are distinct rows of that shard, r * 4096 and up; each shard deletes its first and its last row.
All inputs are finite; a program needn't handle non-finite values.
Results may differ from the reference program's by a relative error of at most 0.015.
Values may be sent and summed in bfloat16 or wider, within the bound.
No kernel may reach another device: no remote copies, remote signals or barrier semaphores. Data moves between devices by JAX's collectives and lax.ppermute only.
A program may use at most 128 MiB of HBM per device.

```python
import jax
import jax.numpy as jnp
from jax import lax

BLK = 128
DIRS = 128
ITERS = 3
RB = 32
FB = 16
NBLK = 256
DEL_DEV = 512
ROWS_DEV = 4096
FEAT_DEV = 2048
ROWS = 16384
FEATURES = 16384
BLOCKS_R = 1024
PANEL = 1024
N_ROW = 4
N_COL = 8


def draw_block_ids(key, part):
    row_shards = ROWS // ROWS_DEV
    column_shards = FEATURES // FEAT_DEV
    subkeys = jax.random.split(key, row_shards * column_shards)

    def choose(subkey):
        inner = jax.random.permutation(subkey, RB * FB - 2)[:NBLK - 2] + 1
        ends = jnp.array([0, RB * FB - 1], dtype=inner.dtype)
        return jnp.sort(jnp.concatenate([ends, inner]))
    chosen = jax.vmap(choose)(subkeys).reshape(row_shards, column_shards, NBLK)
    return jnp.transpose(chosen, (0, 2, 1)).reshape(row_shards * NBLK, column_shards).astype(jnp.int32)


def draw_deleted(key, part):
    row_shards = ROWS // ROWS_DEV
    subkeys = jax.random.split(key, row_shards)

    def choose(subkey):
        inner = jax.random.permutation(subkey, ROWS_DEV - 2)[:DEL_DEV - 2] + 1
        ends = jnp.array([0, ROWS_DEV - 1], dtype=inner.dtype)
        return jnp.concatenate([ends, inner])
    chosen = jax.vmap(choose)(subkeys)
    offsets = (jnp.arange(row_shards) * ROWS_DEV)[:, None]
    return (chosen + offsets).reshape(-1).astype(jnp.int32)


def draw_grads(key, part):
    key_base = jax.random.fold_in(key, 11)
    key_rows = jax.random.fold_in(key, 12)
    key_cols = jax.random.fold_in(key, 13)
    row_scale = jnp.exp(jax.random.uniform(key_rows, (FEATURES, 1), jnp.float32, jnp.log(0.1), 0.0))
    column_scale = jnp.exp(jax.random.uniform(key_cols, (1, DIRS), jnp.float32, jnp.log(0.3), 0.0))
    base = jax.random.normal(key_base, (FEATURES, DIRS), jnp.float32)
    return (jnp.clip(base, -6.0, 6.0) * row_scale * column_scale).astype(jnp.float32)


def block_levels(key, dims, pieces, least, high):
    loudness, own = 1.0, jax.random.fold_in(key, 6)
    for position, blocks in pieces:
        draws = jnp.exp(jax.random.uniform(jax.random.fold_in(own, position), (blocks,), jnp.float32, least / len(pieces), high / len(pieces)))
        loudness = loudness * jnp.repeat(draws, dims[position] // blocks).reshape([-1 if axis == position else 1 for axis in range(len(dims))])
    return loudness


def gaussian(key, shape, width, bound, shards=(), held_as=jnp.bfloat16):
    gain = block_levels(key, shape, shards, -0.22, 0.18) if shards else 1.0
    drawn = jax.random.normal(key, shape, jnp.float32) * width * gain
    return jnp.minimum(jnp.maximum(drawn, -bound), bound).astype(held_as)


def setup_inputs(seed: int = 0) -> dict:
    seeds = jax.random.split(jax.random.key(seed), 6)
    x_blocks = gaussian(seeds[0], (BLOCKS_R, PANEL, BLK), (NBLK * PANEL // RB) ** -0.5, 0.0625, ((0, 4), (1, 8)))
    block_ids = draw_block_ids(jax.random.fold_in(seeds[5], 71), 0)
    margins = gaussian(seeds[2], (ROWS,), 1.5, 6.0, ((0, 4),), jnp.float32)
    deleted = draw_deleted(jax.random.fold_in(seeds[5], 71), 0)
    grads = draw_grads(jax.random.fold_in(seeds[5], 71), 0)
    return dict(x_blocks=x_blocks, block_ids=block_ids, margins=margins, deleted=deleted, grads=grads)


highest = lax.Precision.HIGHEST
ridge_weight = 0.2


def forward_part(blocks, pattern, picked_tiles):
    block_row = pattern // FB
    block_column = pattern % FB
    gathered = picked_tiles[block_column].astype(jnp.float32)
    product = jnp.einsum("bij,bjk->bik", blocks.astype(jnp.float32), gathered, precision=highest)
    select = (block_row[:, None] == jnp.arange(RB, dtype=jnp.int32)[None, :]).astype(jnp.float32)
    return jnp.einsum("br,bik->rik", select, product, precision=highest)


def backward_part(blocks, pattern, scaled):
    block_row = pattern // FB
    block_column = pattern % FB
    gathered = scaled[block_row].astype(jnp.float32)
    product = jnp.einsum("bji,bjk->bik", blocks.astype(jnp.float32), gathered, precision=highest)
    select = (block_column[:, None] == jnp.arange(FB, dtype=jnp.int32)[None, :]).astype(jnp.float32)
    return jnp.einsum("bc,bik->cik", select, product, precision=highest)


def reference(x_blocks, block_ids, margins, deleted, grads):
    blocks = x_blocks.reshape(N_ROW, NBLK, N_COL, BLK, BLK)
    pattern = block_ids.reshape(N_ROW, NBLK, N_COL)
    shard_rows = jnp.arange(ROWS, dtype=jnp.int32).reshape(N_ROW, ROWS_DEV)
    dropped = deleted.reshape(N_ROW, DEL_DEV)
    removed = jnp.any(shard_rows[:, :, None] == dropped[:, None, :], axis=2)
    logistic = jax.nn.sigmoid(margins.reshape(N_ROW, ROWS_DEV))
    weights = jnp.where(removed, 0.0, logistic * (1.0 - logistic)).reshape(N_ROW, RB, BLK, 1)

    def operate(direction):
        picked_tiles = direction.astype(jnp.bfloat16).reshape(N_COL, FB, BLK, DIRS)

        def row_shard(row_index):
            def add_column(column_index, total):
                return total + forward_part(blocks[row_index, :, column_index], pattern[row_index, :, column_index], picked_tiles[column_index])
            return lax.fori_loop(0, N_COL, add_column, jnp.zeros((RB, BLK, DIRS), jnp.float32))

        projected = lax.map(row_shard, jnp.arange(N_ROW, dtype=jnp.int32))
        scaled = (weights * projected).astype(jnp.bfloat16)

        def column_shard(column_index):
            def add_row(row_index, total):
                return total + backward_part(blocks[row_index, :, column_index], pattern[row_index, :, column_index], scaled[row_index])
            return lax.fori_loop(0, N_ROW, add_row, jnp.zeros((FB, BLK, DIRS), jnp.float32))

        backward = lax.map(column_shard, jnp.arange(N_COL, dtype=jnp.int32)).reshape(FEATURES, DIRS)
        return backward + ridge_weight * direction

    solution = jnp.zeros_like(grads)
    residual = grads
    direction = grads
    norm_now = jnp.sum(residual * residual, axis=0)
    for iteration in range(ITERS):
        hessian_image = operate(direction)
        curvature = jnp.sum(direction * hessian_image, axis=0)
        step_size = norm_now / curvature
        solution = solution + step_size * direction
        residual = residual - step_size * hessian_image
        norm_next = jnp.sum(residual * residual, axis=0)
        direction = residual + (norm_next / norm_now) * direction
        norm_now = norm_next
    return solution, residual
```

```python
import functools

import jax
import jax.numpy as jnp
from jax import lax
from jax.experimental import pallas as pl
from jax.experimental.pallas import tpu as pltpu
from jax.sharding import PartitionSpec as P

ITERS = 3
RIDGE = 0.2
GROUP = 16
TAIL = 16

f32 = jnp.float32
bf16 = jnp.bfloat16
VMEM = pl.BlockSpec(memory_space=pltpu.VMEM)
SMEM = pl.BlockSpec(memory_space=pltpu.SMEM)


def tree(values):
    while len(values) > 1:
        values = [values[i] + values[i + 1] for i in range(0, len(values), 2)]
    return values[0]


def to_tail(sums):
    rows = lax.broadcasted_iota(jnp.int32, (TAIL, sums[0].shape[1]), 0)
    tile = jnp.zeros(rows.shape, f32)
    for position, value in enumerate(sums):
        for part in range(3):
            piece = value.astype(bf16).astype(f32)
            tile = jnp.where(rows == 3 * position + part, piece, tile)
            value = value - piece
    return tile.astype(bf16)


def from_tail(tile, position=0):
    start = 3 * position
    return tile[start : start + 1] + tile[start + 1 : start + 2] + tile[start + 2 : start + 3]


def tail_of(ref):
    rows = ref.shape[0]
    return ref[rows - TAIL : rows, :].astype(f32)


def column_sum(value):
    return jnp.sum(value, axis=0, keepdims=True)


def forward_kernel(cfg, tails, *refs):
    pieces = len(refs) - 9
    place, ids, x = refs[:3]
    parts = refs[3 : 3 + pieces]
    send, keep, keep_tail, full, held, total = refs[3 + pieces :]
    fb, rb, nb, zb, width = cfg["fb"], cfg["rb"], cfg["nb"], cfg["zb"], cfg["width"]
    chips = cfg["cols"] // 2
    c, z = place[0], place[1]
    if pieces == 1:
        held[...] = parts[0][...].astype(bf16).reshape(held.shape)
    else:
        for k, part in enumerate(parts):
            held[pl.ds((z ^ k) * zb, zb)] = part[: zb * width, :].reshape((zb, width, -1))
    total[...] = jnp.zeros_like(total)

    def step(i, carry):
        products = []
        for u in range(GROUP):
            k = i * GROUP + u
            a = ids[k] // fb
            b = ids[k] - a * fb
            slot = a // nb
            relative = slot ^ c
            target = ((relative & 1) * chips + (relative >> 1)) * nb + (a - slot * nb)
            products.append((target, jnp.dot(x[k], held[b], preferred_element_type=f32)))
        for target, product in products:
            total[target] = total[target] + product
        return carry

    lax.fori_loop(0, x.shape[0] // GROUP, step, 0)
    half = rb // 2
    rows = half * width
    keep[...] = total[:half].reshape(keep.shape)
    send[:rows, :] = total[half:].reshape(keep.shape).astype(bf16)
    if tails:
        tile = to_tail([from_tail(tree([tail_of(part) for part in parts]))])
        send[rows:, :] = tile
        keep_tail[...] = tile
    else:
        send[rows:, :] = jnp.zeros((TAIL, send.shape[1]), bf16)
        keep_tail[...] = jnp.zeros(keep_tail.shape, bf16)
    if pieces > 1:
        full[...] = held[...].reshape(full.shape)
    else:
        full[...] = jnp.zeros_like(full)


def merge_kernel(cfg, *refs):
    keep, keep_tail, received, own, own_tail = refs[:5]
    sends = refs[5:]
    rows = cfg["nb"] * cfg["width"]
    tile = keep_tail[...].astype(f32) + tail_of(received)
    tile = to_tail([from_tail(tile)])
    own[...] = keep[:rows, :] + received[:rows, :].astype(f32)
    own_tail[...] = tile
    for k, send in enumerate(sends, start=1):
        span = slice(k * rows, (k + 1) * rows)
        send[:rows, :] = (keep[span, :] + received[span, :].astype(f32)).astype(bf16)
        send[rows:, :] = tile


def scale_kernel(cfg, first, *refs):
    chips = cfg["cols"] // 2
    own, own_tail = refs[:2]
    received = refs[2 : 1 + chips]
    rest = refs[1 + chips :]
    rows = own.shape[0]
    projected = tree([own[...]] + [r[:rows, :].astype(f32) for r in received])
    if first:
        weights, direction, scaled, kept, spread = rest
        width = cfg["width"]
        for j in range(cfg["nb"]):
            row = jnp.broadcast_to(weights[j : j + 1, :], (width, width))
            spread[j * width : (j + 1) * width, :] = row.T
        d = direction[...]
        norm = column_sum(d * d)
    else:
        spread, residual, old, before, norm_now, scaled, kept, direction, norm_out, beta_out = rest
        tile = tree([own_tail[...].astype(f32)] + [tail_of(r) for r in received])
        norm = from_tail(tile)
        beta = norm / norm_now[0:1, :]
        projected = projected + beta * before[...]
        d = residual[...] + beta * old[...]
        direction[...] = d
        norm_out[...] = jnp.broadcast_to(norm, norm_out.shape)
        beta_out[...] = jnp.broadcast_to(beta, beta_out.shape)
    kept[...] = projected
    weighted = spread[...] * projected
    scaled[:rows, :] = weighted.astype(bf16)
    curvature = column_sum(weighted * projected) + RIDGE * column_sum(d * d)
    scaled[rows:, :] = to_tail([curvature, norm] if first else [curvature])


def backward_kernel(cfg, first, *refs):
    cols, rows_axis = cfg["cols"], cfg["rows"]
    place, ids, x = refs[:3]
    parts = refs[3 : 3 + cols]
    own, own_tail = refs[3 + cols : 5 + cols]
    sends = refs[5 + cols : 4 + cols + rows_axis]
    held, total = refs[4 + cols + rows_axis :]
    fb, nb, zb, width = cfg["fb"], cfg["nb"], cfg["zb"], cfg["width"]
    c, z = place[0], place[1]
    for k, part in enumerate(parts):
        held[pl.ds((c ^ k) * nb, nb)] = part[: nb * width, :].reshape((nb, width, -1))
    total[...] = jnp.zeros_like(total)

    def step(i, carry):
        products = []
        for u in range(GROUP):
            k = i * GROUP + u
            a = ids[k] // fb
            b = ids[k] - a * fb
            slot = b // zb
            target = (slot ^ z) * zb + (b - slot * zb)
            product = lax.dot_general(
                x[k], held[a], (((0,), (0,)), ((), ())), preferred_element_type=f32
            )
            products.append((target, product))
        for target, product in products:
            total[target] = total[target] + product
        return carry

    lax.fori_loop(0, x.shape[0] // GROUP, step, 0)
    tile = tree([tail_of(part) for part in parts])
    tile = to_tail([from_tail(tile, j) for j in range(2 if first else 1)])
    span = zb * width
    own[...] = total[:zb].reshape(own.shape)
    own_tail[...] = tile
    for k, send in enumerate(sends, start=1):
        send[:span, :] = total[k * zb : (k + 1) * zb].reshape(own.shape).astype(bf16)
        send[span:, :] = tile


def update_kernel(cfg, first, *refs):
    others = cfg["rows"] - 1
    own, own_tail = refs[:2]
    received = refs[2 : 2 + others]
    direction, residual, norm_now, share, after, norm_out, alpha_out = refs[2 + others :]
    rows = own.shape[0]
    image = tree([own[...]] + [r[:rows, :].astype(f32) for r in received])
    image = image + RIDGE * direction[...]
    tile = tree([own_tail[...].astype(f32)] + [tail_of(r) for r in received])
    norm = from_tail(tile, 1) if first else norm_now[0:1, :]
    alpha = norm / from_tail(tile)
    left = residual[...] - alpha * image
    after[...] = left
    norm_out[...] = jnp.broadcast_to(norm, norm_out.shape)
    alpha_out[...] = jnp.broadcast_to(alpha, alpha_out.shape)
    share[:rows, :] = left.astype(bf16)
    share[rows:, :] = to_tail([column_sum(left * left)])


def result_kernel(count, *refs):
    grads = refs[0]
    residuals = refs[1:count]
    alphas = refs[count : 2 * count]
    betas = refs[2 * count : 3 * count - 1]
    out = refs[3 * count - 1]
    d = grads[...]
    total = alphas[0][0:1, :] * d
    for j in range(1, count):
        d = residuals[j - 1][...].astype(f32) + betas[j - 1][0:1, :] * d
        total = total + alphas[j][0:1, :] * d
    out[...] = total


def on_device(cfg, x_blocks, block_ids, margins, deleted, grads):
    width = x_blocks.shape[1]
    directions = grads.shape[1]
    cols, rows_axis = cfg["cols"], cfg["rows"]
    rb, fb = margins.shape[0] // width, grads.shape[0] // width
    nb, zb = rb // cols, fb // rows_axis
    cfg = dict(cfg, rb=rb, fb=fb, nb=nb, zb=zb, width=width)
    c, z = lax.axis_index("col"), lax.axis_index("row")
    place = jnp.stack([c, z]).astype(jnp.int32)
    ids = block_ids[:, 0]
    own_rows, own_features = nb * width, zb * width
    chips = cols // 2

    def shape(rows, dtype):
        return jax.ShapeDtypeStruct((rows, directions), dtype)

    def along_col(value, k):
        return lax.ppermute(value, "col", [(i, i ^ k) for i in range(cols)])

    def along_row(value, k):
        return lax.ppermute(value, "row", [(i, i ^ k) for i in range(rows_axis)])

    def call(kernel, out, inputs, smem=0, scratch=()):
        return pl.pallas_call(
            kernel,
            out_shape=out,
            in_specs=[SMEM] * smem + [VMEM] * (len(inputs) - smem),
            out_specs=[VMEM] * len(out),
            scratch_shapes=list(scratch),
        )(*inputs)

    row_ids = z * margins.shape[0] + c * own_rows + jnp.arange(own_rows, dtype=jnp.int32)
    row_ids = row_ids.reshape(nb, width)
    removed = jnp.any(row_ids[None] == deleted[:, None, None], axis=0)
    logistic = jax.nn.sigmoid(lax.dynamic_slice_in_dim(margins, c * own_rows, own_rows))
    logistic = logistic.reshape(nb, width)
    weights = jnp.where(removed, 0.0, logistic * (1.0 - logistic))

    residual = direction = lax.dynamic_slice_in_dim(grads, z * own_features, own_features)
    parts = [grads]
    residuals, alphas, betas = [], [], []
    norm_now = spread = before = None
    for iteration in range(ITERS):
        first = iteration == 0
        send, keep, keep_tail, full = call(
            functools.partial(forward_kernel, cfg, not first),
            [
                shape(rb // 2 * width + TAIL, bf16),
                shape(rb // 2 * width, f32),
                shape(TAIL, bf16),
                shape(fb * width if not first else TAIL, bf16),
            ],
            [place, ids, x_blocks, *parts],
            smem=2,
            scratch=[
                pltpu.VMEM((fb, width, directions), bf16),
                pltpu.VMEM((rb, width, directions), f32),
            ],
        )
        if not first:
            residuals.append(full)
        received = along_col(send, 1)
        own, own_tail, *sends = call(
            functools.partial(merge_kernel, cfg),
            [shape(own_rows, f32), shape(TAIL, bf16)]
            + [shape(own_rows + TAIL, bf16)] * (chips - 1),
            [keep, keep_tail, received],
        )
        received = [along_col(send, 2 * k) for k, send in enumerate(sends, start=1)]
        if first:
            scaled, before, spread = call(
                functools.partial(scale_kernel, cfg, True),
                [shape(own_rows + TAIL, bf16), shape(own_rows, f32), shape(own_rows, f32)],
                [own, own_tail, *received, weights, direction],
            )
        else:
            scaled, before, direction, norm_now, beta = call(
                functools.partial(scale_kernel, cfg, False),
                [
                    shape(own_rows + TAIL, bf16),
                    shape(own_rows, f32),
                    shape(own_features, f32),
                    shape(8, f32),
                    shape(8, f32),
                ],
                [own, own_tail, *received, spread, residual, direction, before, norm_now],
            )
            betas.append(beta)
        chip_parts = [scaled] + [along_col(scaled, 2 * k) for k in range(1, chips)]
        parts = [p for part in chip_parts for p in (part, along_col(part, 1))]
        own, own_tail, *sends = call(
            functools.partial(backward_kernel, cfg, first),
            [shape(own_features, f32), shape(TAIL, bf16)]
            + [shape(own_features + TAIL, bf16)] * (rows_axis - 1),
            [place, ids, x_blocks, *parts],
            smem=2,
            scratch=[
                pltpu.VMEM((rb, width, directions), bf16),
                pltpu.VMEM((fb, width, directions), f32),
            ],
        )
        received = [along_row(send, k) for k, send in enumerate(sends, start=1)]
        if first:
            norm_now = jnp.zeros((8, directions), f32)
        share, residual, norm_now, alpha = call(
            functools.partial(update_kernel, cfg, first),
            [
                shape(own_features + TAIL, bf16),
                shape(own_features, f32),
                shape(8, f32),
                shape(8, f32),
            ],
            [own, own_tail, *received, direction, residual, norm_now],
        )
        alphas.append(alpha)
        parts = [share] + [along_row(share, k) for k in range(1, rows_axis)]
    (answer,) = call(
        functools.partial(result_kernel, ITERS),
        [shape(fb * width, f32)],
        [grads, *residuals, *alphas, *betas],
    )
    left = jnp.zeros((rows_axis, own_features, directions), f32)
    left = jnp.stack([p[:own_features].astype(f32) for p in parts])
    order = jnp.arange(rows_axis, dtype=jnp.int32) ^ z
    left = left[order].reshape(fb * width, directions)
    return (answer, left)


def solution(mesh):
    cfg = {"rows": mesh.shape["row"], "cols": mesh.shape["col"]}
    placed = (P("row", "col", None), P("row", "col"), P("row"), P("row"), P("col", None))
    return jax.shard_map(
        functools.partial(on_device, cfg),
        mesh=mesh,
        in_specs=placed,
        out_specs=(P("col", None), P("col", None)),
        check_vma=False,
    )
```

```python
import functools

import jax
import jax.numpy as jnp
from jax import lax
from jax.experimental import pallas as pl
from jax.experimental.pallas import tpu as pltpu
from jax.sharding import PartitionSpec as P


ITERS = 3
RIDGE = 0.2
TAIL = 16

GROUP = 8
CHUNKS = 8


def row_order(n):
    return list(range(1, n))


def row_groups(n):
    return [[k] for k in range(n)]


def chip_order(n):
    return list(range(1, n))


def column_groups(n):
    order = chip_order(n)
    between = [[2 * before + 1, 2 * k] for before, k in zip(order, order[1:])]
    return [[0, 1], [2 * order[0]], *between, [2 * order[-1] + 1]]


f32 = jnp.float32
bf16 = jnp.bfloat16
VMEM = pl.BlockSpec(memory_space=pltpu.VMEM)


def tree(values):
    while len(values) > 1:
        values = [values[i] + values[i + 1] for i in range(0, len(values), 2)]
    return values[0]


def to_tail(sums):
    rows = lax.broadcasted_iota(jnp.int32, (TAIL, sums[0].shape[1]), 0)
    tile = jnp.zeros(rows.shape, f32)
    for position, value in enumerate(sums):
        for part in range(3):
            piece = value.astype(bf16).astype(f32)
            tile = jnp.where(rows == 3 * position + part, piece, tile)
            value = value - piece
    return tile.astype(bf16)


def from_tail(tile, position=0):
    start = 3 * position
    return tile[start : start + 1] + tile[start + 1 : start + 2] + tile[start + 2 : start + 3]


def tail_of(ref):
    rows = ref.shape[0]
    return ref[rows - TAIL : rows, :].astype(f32)


def column_sum(value):
    return jnp.sum(value, axis=0, keepdims=True)


def here():
    return lax.axis_index("col"), lax.axis_index("row")


def place_of(cfg, relative):
    return (relative & 1) * (cfg["cols"] // 2) + (relative >> 1)


def first_kernel(
    cfg,
    ids_far,
    listed,
    far,
    send,
    keep,
    keep_tail,
    direction,
    ids,
    x,
    near,
    held,
    total,
    arrived,
):
    fb, nb = cfg["fb"], cfg["nb"]
    c, z = here()
    count = ids.shape[0]
    size = count // CHUNKS
    numbers = pltpu.make_async_copy(ids_far, ids, arrived.at[CHUNKS + 1])
    head = pltpu.make_async_copy(far, near, arrived.at[CHUNKS])
    numbers.start()
    head.start()
    copies = [
        pltpu.make_async_copy(
            listed.at[pl.ds(i * size, size)], x.at[pl.ds(i * size, size)], arrived.at[i]
        )
        for i in range(CHUNKS)
    ]
    for copy in copies:
        copy.start()
    total[...] = jnp.zeros_like(total)
    numbers.wait()
    head.wait()
    own = direction.shape[0]
    direction[...] = near[pl.ds(pl.multiple_of(z * own, own), own), :]
    held[...] = near[...].astype(bf16).reshape(held.shape)
    for i, copy in enumerate(copies):
        copy.wait()

        def step(j, carry, i=i):
            products = []
            for u in range(GROUP):
                k = i * size + j * GROUP + u
                a = ids[k] // fb
                b = ids[k] - a * fb
                slot = a // nb
                target = place_of(cfg, slot ^ c) * nb + (a - slot * nb)
                products.append((target, jnp.dot(x[k], held[b], preferred_element_type=f32)))
            for target, product in products:
                total[target] = total[target] + product
            return carry

        lax.fori_loop(0, size // GROUP, step, 0)
    half = total.shape[0] // 2
    rows = keep.shape[0]
    keep[...] = total[:half].reshape(keep.shape)
    send[:rows, :] = total[half:].reshape(keep.shape).astype(bf16)
    send[rows:, :] = jnp.zeros((TAIL, send.shape[1]), bf16)
    keep_tail[...] = jnp.zeros(keep_tail.shape, bf16)


def dense_kernel(cfg, ids_far, listed, dense, ids, x, arrived):
    fb, zb, width = cfg["fb"], cfg["zb"], cfg["width"]
    size = x.shape[0] // CHUNKS
    copies = [
        pltpu.make_async_copy(
            listed.at[pl.ds(i * size, size)], x.at[pl.ds(i * size, size)], arrived.at[i]
        )
        for i in range(CHUNKS)
    ]
    numbers = pltpu.make_async_copy(ids_far, ids, arrived.at[CHUNKS])
    numbers.start()
    for copy in copies:
        copy.start()

    def clear(a, carry):
        rows = pl.ds(pl.multiple_of(a * width, width), width)
        dense[:, rows, :] = jnp.zeros((dense.shape[0], width, dense.shape[2]), bf16)
        return carry

    lax.fori_loop(0, cfg["rb"], clear, 0)
    numbers.wait()
    for i, copy in enumerate(copies):
        copy.wait()

        def step(j, carry, i=i):
            for u in range(GROUP):
                k = i * size + j * GROUP + u
                a = ids[k] // fb
                b = ids[k] - a * fb
                h = b // zb
                down = pl.ds(pl.multiple_of(a * width, width), width)
                across = pl.ds(pl.multiple_of((b - h * zb) * width, width), width)
                dense[h, down, across] = x[k]
            return carry

        lax.fori_loop(0, size // GROUP, step, 0)


def forward_kernel(cfg, group, x, *refs):
    parts, total = refs[: len(group)], refs[-1]
    rows = cfg["nb"] * cfg["width"]

    for i in range(cfg["cols"]):
        span = slice(i * rows, (i + 1) * rows)
        product = sum(
            jnp.dot(
                x[here()[1] ^ g, span, :], part[: x.shape[2], :], preferred_element_type=f32
            )
            for g, part in zip(group, parts)
        )
        if len(refs) > len(group) + 1:
            product = refs[len(group)][span, :] + product
        total[span, :] = product


def forward_last_kernel(cfg, group, sent, x, *refs):
    parts = refs[: cfg["rows"]]
    total, out = refs[cfg["rows"] : cfg["rows"] + 2]
    rows = cfg["nb"] * cfg["width"]
    chips = cfg["cols"] // 2
    for i in range(chips):
        slot = (2 * i + (1 if sent else 0)) ^ here()[0]
        span = pl.ds(pl.multiple_of(slot * rows, rows), rows)
        value = total[span, :]
        for g in group:
            value = value + jnp.dot(
                x[here()[1] ^ g, span, :], parts[g][: x.shape[2], :], preferred_element_type=f32
            )
        out[i * rows : (i + 1) * rows, :] = value.astype(out.dtype)
    if sent:
        tile = to_tail([from_tail(tree([tail_of(part) for part in parts]))])
        out[chips * rows :, :] = tile
        refs[-1][...] = tile


def merge_kernel(cfg, *refs):
    keep, keep_tail, received = refs[:3]
    own, own_tail, *sends = refs[3:]
    rows = cfg["nb"] * cfg["width"]
    tile = keep_tail[...].astype(f32) + tail_of(received)
    tile = to_tail([from_tail(tile)])
    own[...] = keep[:rows, :] + received[:rows, :].astype(f32)
    own_tail[...] = tile
    for k, send in enumerate(sends, start=1):
        span = slice(k * rows, (k + 1) * rows)
        send[:rows, :] = (keep[span, :] + received[span, :].astype(f32)).astype(bf16)
        send[rows:, :] = tile


def scale_kernel(cfg, first, *refs):
    chips = cfg["cols"] // 2
    own, own_tail = refs[:2]
    received = refs[2 : 1 + chips]
    rest = refs[1 + chips :]
    rows = own.shape[0]
    projected = tree([own[...]] + [r[:rows, :].astype(f32) for r in received])
    if first:
        removed, margins, direction, scaled, kept, spread = rest
        width = cfg["width"]
        for j in range(cfg["nb"]):
            logistic = 1.0 / (1.0 + jnp.exp(-margins[pl.ds(here()[0] * cfg["nb"] + j, 1), :]))
            weight = jnp.where(removed[j : j + 1, :] > 0.0, 0.0, logistic * (1.0 - logistic))
            row = jnp.broadcast_to(weight, (width, width))
            spread[j * width : (j + 1) * width, :] = row.T
        d = direction[...]
        norm = column_sum(d * d)
    else:
        spread, residual, old, before, norm_now, scaled, kept, direction, norm_out, beta_out = rest
        tile = tree([own_tail[...].astype(f32)] + [tail_of(r) for r in received])
        norm = from_tail(tile)
        beta = norm / norm_now[0:1, :]
        projected = projected + beta * before[...]
        d = residual[...] + beta * old[...]
        direction[...] = d
        norm_out[...] = jnp.broadcast_to(norm, norm_out.shape)
        beta_out[...] = jnp.broadcast_to(beta, beta_out.shape)
    kept[...] = projected
    weighted = spread[...] * projected
    width = cfg["width"]
    for j in range(cfg["nb"]):
        tile = weighted[j * width : (j + 1) * width, :]
        scaled[j * width : (j + 1) * width, :] = tile.T.astype(bf16)
    curvature = column_sum(weighted * projected) + RIDGE * column_sum(d * d)
    scaled[rows:, :] = to_tail([curvature, norm] if first else [curvature])


def turned(cfg, part):
    width = cfg["width"]
    return jnp.concatenate(
        [part[j * width : (j + 1) * width, :] for j in range(cfg["nb"])], axis=1
    )


def backward_sum(cfg, group, x, near, h):
    rows = cfg["nb"] * cfg["width"]
    products = []
    for g, part in zip(group, near):
        span = pl.ds(pl.multiple_of((here()[0] ^ g) * rows, rows), rows)
        products.append(jnp.dot(part, x[h, span, :], preferred_element_type=f32))
    return sum(products)


def backward_kernel(cfg, group, x, *refs):
    near = [turned(cfg, part) for part in refs[: len(group)]]
    total = refs[-1]
    for h in range(cfg["rows"]):
        product = backward_sum(cfg, group, x, near, h)
        if len(refs) > len(group) + 1:
            product = refs[len(group)][h] + product
        total[h] = product


def backward_last_kernel(cfg, group, first, sent, x, *refs):
    cols, width = cfg["cols"], cfg["width"]
    parts, total = refs[:cols], refs[cols]
    near = [turned(cfg, parts[g]) for g in group]
    outs = refs[cols + 1 :]
    if sent:
        tile = tree([tail_of(part) for part in parts])
        tile = to_tail([from_tail(tile, j) for j in range(2 if first else 1)])
        outs[-1][...] = tile
    for k in range(1, cfg["rows"]) if sent else [0]:
        out = outs[k - 1] if sent else outs[0]
        h = here()[1] ^ k
        value = total[h] + backward_sum(cfg, group, x, near, h)
        for j in range(cfg["zb"]):
            out[j * width : (j + 1) * width, :] = value[:, j * width : (j + 1) * width].astype(
                out.dtype
            )
        if sent:
            out[cfg["zb"] * width :, :] = tile


def update_kernel(cfg, first, *refs):
    others = cfg["rows"] - 1
    own, own_tail = refs[:2]
    received = refs[2 : 2 + others]
    direction, residual, norm_now, share, after, norm_out, alpha_out = refs[2 + others :]
    rows = own.shape[0]
    image = tree([own[...]] + [r[:rows, :].astype(f32) for r in received])
    width = cfg["width"]
    image = [image[j * width : (j + 1) * width, :].T for j in range(cfg["zb"])]
    image = jnp.concatenate(image, axis=0) + RIDGE * direction[...]
    tile = tree([own_tail[...].astype(f32)] + [tail_of(r) for r in received])
    norm = from_tail(tile, 1) if first else norm_now[0:1, :]
    alpha = norm / from_tail(tile)
    left = residual[...] - alpha * image
    after[...] = left
    norm_out[...] = jnp.broadcast_to(norm, norm_out.shape)
    alpha_out[...] = jnp.broadcast_to(alpha, alpha_out.shape)
    share[:rows, :] = left.astype(bf16)
    share[rows:, :] = to_tail([column_sum(left * left)])


def result_kernel(cfg, count, *refs):
    others = cfg["rows"]
    grads = refs[0]
    shares = refs[1 : 1 + others * (count - 1)]
    rest = refs[1 + len(shares) :]
    alphas, betas, out = rest[:count], rest[count : 2 * count - 1], rest[-1]
    rows = grads.shape[0] // others
    for k in range(others):
        span = pl.ds(pl.multiple_of((here()[1] ^ k) * rows, rows), rows)
        d = grads[span, :]
        total = alphas[0][0:1, :] * d
        for j in range(1, count):
            share = shares[(j - 1) * others + k]
            d = share[:rows, :].astype(f32) + betas[j - 1][0:1, :] * d
            total = total + alphas[j][0:1, :] * d
        out[span, :] = total


def residual_kernel(cfg, *refs):
    shares, out = refs[:-1], refs[-1]
    rows = out.shape[0] // cfg["rows"]
    for k, share in enumerate(shares):
        span = pl.ds(pl.multiple_of((here()[1] ^ k) * rows, rows), rows)
        out[span, :] = share[:rows, :].astype(f32)


def on_device(cfg, x_blocks, block_ids, margins, deleted, grads):
    width = x_blocks.shape[1]
    directions = grads.shape[1]
    cols, rows_axis = cfg["cols"], cfg["rows"]
    rb, fb = margins.shape[0] // width, grads.shape[0] // width
    nb, zb = rb // cols, fb // rows_axis
    cfg = dict(cfg, rb=rb, fb=fb, nb=nb, zb=zb, width=width)
    c, z = lax.axis_index("col"), lax.axis_index("row")
    ids = block_ids[:, 0]
    own_rows, own_features = nb * width, zb * width
    chips = cols // 2
    half = rb // 2 * width

    def shape(rows, dtype):
        return jax.ShapeDtypeStruct((rows, directions), dtype)

    def along(axis, value, k):
        n = rows_axis if axis == "row" else cols
        return lax.ppermute(value, axis, [(i, i ^ k) for i in range(n)])

    def exchange(axis, values, order, step=1):
        received = {k: along(axis, values[k - 1], step * k) for k in order}
        return [received[k] for k in range(1, len(order) + 1)]

    def near(value):
        return pltpu.with_memory_space_constraint(value, pltpu.VMEM)

    def far(value):
        return pltpu.with_memory_space_constraint(value, pltpu.HBM)

    def call(kernel, out, inputs, stay=True, aliases=None):
        if stay:
            out = [pltpu.VMEM(o.shape, o.dtype) for o in out]
        return pl.pallas_call(
            kernel,
            out_shape=out,
            in_specs=[VMEM] * len(inputs),
            out_specs=[VMEM] * len(out),
            input_output_aliases=aliases or {},
            compiler_params=pltpu.CompilerParams(vmem_limit_bytes=4 << 20),
        )(*map(near, inputs))

    matrix = []

    def multiply(kernel, out, inputs, aliases=None):
        at = len(inputs)

        def body(*refs):
            kernel(refs[at], *refs[:at], *refs[at + 1 : -1])

        x = matrix.pop()
        *results, x = call(
            body,
            [*out, jax.ShapeDtypeStruct(x.shape, x.dtype)],
            [*inputs, x],
            aliases={**(aliases or {}), at: len(out)},
        )
        matrix.append(x)
        return results

    def begin():
        return pl.pallas_call(
            functools.partial(first_kernel, cfg),
            out_shape=[
                pltpu.VMEM((half + TAIL, directions), bf16),
                pltpu.VMEM((half, directions), f32),
                pltpu.VMEM((TAIL, directions), bf16),
                pltpu.VMEM((own_features, directions), f32),
            ],
            in_specs=[pl.BlockSpec(memory_space=pltpu.HBM)] * 3,
            out_specs=[VMEM] * 4,
            scratch_shapes=[
                pltpu.SMEM(ids.shape, jnp.int32),
                pltpu.VMEM(x_blocks.shape, bf16),
                pltpu.VMEM(grads.shape, f32),
                pltpu.VMEM((fb, width, directions), bf16),
                pltpu.VMEM((rb, width, directions), f32),
                pltpu.SemaphoreType.DMA((CHUNKS + 2,)),
            ],
            compiler_params=pltpu.CompilerParams(vmem_limit_bytes=16 << 20),
        )(far(ids), far(x_blocks), far(grads))

    def lay_out():
        return pl.pallas_call(
            functools.partial(dense_kernel, cfg),
            out_shape=pltpu.VMEM((rows_axis, rb * width, own_features), bf16),
            in_specs=[pl.BlockSpec(memory_space=pltpu.HBM)] * 2,
            out_specs=VMEM,
            scratch_shapes=[
                pltpu.SMEM(ids.shape, jnp.int32),
                pltpu.VMEM(x_blocks.shape, bf16),
                pltpu.SemaphoreType.DMA((CHUNKS + 1,)),
            ],
            compiler_params=pltpu.CompilerParams(vmem_limit_bytes=12 << 20),
        )(far(ids), far(x_blocks))

    def forward(parts):
        total = []
        *groups, group = row_groups(rows_axis)
        for some in groups:
            total = multiply(
                functools.partial(forward_kernel, cfg, some),
                [shape(rb * width, f32)],
                [parts[g] for g in some] + total,
                aliases={len(some): 0} if total else {},
            )
        send, keep_tail = multiply(
            functools.partial(forward_last_kernel, cfg, group, True),
            [shape(half + TAIL, bf16), shape(TAIL, bf16)],
            [*parts, *total],
        )
        (keep,) = multiply(
            functools.partial(forward_last_kernel, cfg, group, False),
            [shape(half, f32)],
            [*parts, *total],
        )
        return send, keep, keep_tail

    def backward(scaled, first):
        others = exchange("col", [scaled] * (chips - 1), chip_order(chips), 2)
        parts = []
        for part in [scaled, *others]:
            parts += [part, along("col", part, 1)]
        total = []
        *groups, group = column_groups(chips)
        for some in groups:
            total = multiply(
                functools.partial(backward_kernel, cfg, some),
                [jax.ShapeDtypeStruct((rows_axis, directions, own_features), f32)],
                [parts[g] for g in some] + total,
                aliases={len(some): 0} if total else {},
            )
        *sends, own_tail = multiply(
            functools.partial(backward_last_kernel, cfg, group, first, True),
            [shape(own_features + TAIL, bf16)] * (rows_axis - 1) + [shape(TAIL, bf16)],
            [*parts, *total],
        )
        (own,) = multiply(
            functools.partial(backward_last_kernel, cfg, group, first, False),
            [shape(own_features, f32)],
            [*parts, *total],
        )
        return sends, own, own_tail

    row_ids = z * margins.shape[0] + c * own_rows + jnp.arange(own_rows, dtype=jnp.int32)
    row_ids = row_ids.reshape(nb, width)
    removed = jnp.any(row_ids[None] == deleted[:, None, None], axis=0)
    removed = removed.astype(f32)
    margins = margins.reshape(rb, width)
    parts, shares, alphas, betas = [], [], [], []
    share = spread = before = None
    norm_now = jnp.zeros((8, directions), f32)
    for iteration in range(ITERS):
        first = iteration == 0
        if first:
            send, keep, keep_tail, direction = begin()
            residual = direction
        else:
            parts = [share, *exchange("row", [share] * (rows_axis - 1), row_order(rows_axis))]
            shares += parts
            send, keep, keep_tail = forward(parts)
        received = along("col", send, 1)
        own, own_tail, *sends = call(
            functools.partial(merge_kernel, cfg),
            [shape(own_rows, f32), shape(TAIL, bf16)]
            + [shape(own_rows + TAIL, bf16)] * (chips - 1),
            [keep, keep_tail, received],
        )
        received = exchange("col", sends, chip_order(chips), 2)
        if first:
            matrix.append(lay_out())
            scaled, before, spread = call(
                functools.partial(scale_kernel, cfg, True),
                [shape(own_rows + TAIL, bf16), shape(own_rows, f32), shape(own_rows, f32)],
                [own, own_tail, *received, removed, margins, direction],
            )
        else:
            scaled, before, direction, norm_now, beta = call(
                functools.partial(scale_kernel, cfg, False),
                [
                    shape(own_rows + TAIL, bf16),
                    shape(own_rows, f32),
                    shape(own_features, f32),
                    shape(8, f32),
                    shape(8, f32),
                ],
                [own, own_tail, *received, spread, residual, direction, before, norm_now],
            )
            betas.append(beta)
        sends, own, own_tail = backward(scaled, first)
        received = exchange("row", sends, row_order(rows_axis))
        share, residual, norm_now, alpha = call(
            functools.partial(update_kernel, cfg, first),
            [
                shape(own_features + TAIL, bf16),
                shape(own_features, f32),
                shape(8, f32),
                shape(8, f32),
            ],
            [own, own_tail, *received, direction, residual, norm_now],
        )
        alphas.append(alpha)
    parts = [share, *exchange("row", [share] * (rows_axis - 1), row_order(rows_axis))]
    (answer,) = call(
        functools.partial(result_kernel, cfg, ITERS),
        [shape(fb * width, f32)],
        [grads, *shares, *alphas, *betas],
        stay=False,
    )
    (left,) = call(
        functools.partial(residual_kernel, cfg), [shape(fb * width, f32)], parts, stay=False
    )
    return (answer, left)


def solution(mesh):
    cfg = {"rows": mesh.shape["row"], "cols": mesh.shape["col"]}
    placed = (P("row", "col", None), P("row", "col"), P("row"), P("row"), P("col", None))
    return jax.shard_map(
        functools.partial(on_device, cfg),
        mesh=mesh,
        in_specs=placed,
        out_specs=(P("col", None), P("col", None)),
        check_vma=False,
    )
```

```python
import functools

import jax
import jax.numpy as jnp
from jax import lax
from jax.experimental import pallas as pl
from jax.experimental.pallas import tpu as pltpu
from jax.sharding import PartitionSpec as P


ITERS = 3
RIDGE = 0.2
TAIL = 16

GROUP = 32
CHUNKS = 8


def crossed(k, n):
    return (k & ~3) | ((k & 1) << 1) | ((k >> 1) & 1) if n > 2 else k


def row_partners(n):
    basis = [n - 1, *(1 << b for b in range(n.bit_length() - 2))]
    order = [0]
    for value in basis:
        order += [k ^ value for k in order]
    return order


def partner(order, i, odd):
    k = order[i]
    return k + odd * (crossed(k, len(order)) - k)


def row_order(n):
    return list(range(1, n))


def row_groups(n):
    return [[k] for k in range(n)]


def chip_order(n):
    return list(range(1, n))


def column_groups(n):
    order = chip_order(n)
    between = [[2 * before + 1, 2 * k] for before, k in zip(order, order[1:])]
    return [[0, 1], [2 * order[0]], *between, [2 * order[-1] + 1]]


f32 = jnp.float32
bf16 = jnp.bfloat16
VMEM = pl.BlockSpec(memory_space=pltpu.VMEM)


def tree(values):
    while len(values) > 1:
        values = [values[i] + values[i + 1] for i in range(0, len(values), 2)]
    return values[0]


def to_tail(sums):
    rows = lax.broadcasted_iota(jnp.int32, (TAIL, sums[0].shape[1]), 0)
    tile = jnp.zeros(rows.shape, f32)
    for position, value in enumerate(sums):
        for part in range(3):
            piece = value.astype(bf16).astype(f32)
            tile = jnp.where(rows == 3 * position + part, piece, tile)
            value = value - piece
    return tile.astype(bf16)


def from_tail(tile, position=0):
    start = 3 * position
    return tile[start : start + 1] + tile[start + 1 : start + 2] + tile[start + 2 : start + 3]


def tail_of(ref):
    rows = ref.shape[0]
    return ref[rows - TAIL : rows, :].astype(f32)


def column_sum(value):
    return jnp.sum(value, axis=0, keepdims=True)


def here():
    return lax.axis_index("col"), lax.axis_index("row")


def row_slot(cfg, i):
    c, z = here()
    return z ^ partner(row_partners(cfg["rows"]), i, c & 1)


def column_slot(cfg, i, across):
    c = here()[0] ^ across
    return c ^ (2 * partner(range(cfg["cols"] // 2), i, c & 1))


def first_kernel(
    cfg,
    ids_far,
    listed,
    far,
    send,
    keep,
    keep_tail,
    direction,
    ids,
    places,
    x,
    near,
    held,
    total,
    arrived,
):
    fb, nb = cfg["fb"], cfg["nb"]
    chips = cfg["cols"] // 2
    for across in range(2):
        for i in range(chips):
            places[column_slot(cfg, i, across)] = across * chips + i
    z = here()[1]
    count = ids.shape[0]
    size = count // CHUNKS
    numbers = pltpu.make_async_copy(ids_far, ids, arrived.at[CHUNKS + 1])
    head = pltpu.make_async_copy(far, near, arrived.at[CHUNKS])
    numbers.start()
    head.start()
    copies = [
        pltpu.make_async_copy(
            listed.at[pl.ds(i * size, size)], x.at[pl.ds(i * size, size)], arrived.at[i]
        )
        for i in range(CHUNKS)
    ]
    for copy in copies:
        copy.start()
    total[...] = jnp.zeros_like(total)
    numbers.wait()
    head.wait()
    own = direction.shape[0]
    direction[...] = near[pl.ds(pl.multiple_of(z * own, own), own), :]
    held[...] = near[...].astype(bf16).reshape(held.shape)
    for i, copy in enumerate(copies):
        copy.wait()

        def step(j, carry, i=i):
            products = []
            for u in range(GROUP):
                k = i * size + j * GROUP + u
                a = ids[k] // fb
                b = ids[k] - a * fb
                slot = a // nb
                target = places[slot] * nb + (a - slot * nb)
                products.append((target, jnp.dot(x[k], held[b], preferred_element_type=f32)))
            for target, product in products:
                total[target] = total[target] + product
            return carry

        lax.fori_loop(0, size // GROUP, step, 0)
    half = total.shape[0] // 2
    rows = keep.shape[0]
    keep[...] = total[:half].reshape(keep.shape)
    send[:rows, :] = total[half:].reshape(keep.shape).astype(bf16)
    send[rows:, :] = jnp.zeros((TAIL, send.shape[1]), bf16)
    keep_tail[...] = jnp.zeros(keep_tail.shape, bf16)


def dense_kernel(cfg, ids_far, listed, dense, ids, x, arrived):
    fb, zb, width = cfg["fb"], cfg["zb"], cfg["width"]
    size = x.shape[0] // CHUNKS
    copies = [
        pltpu.make_async_copy(
            listed.at[pl.ds(i * size, size)], x.at[pl.ds(i * size, size)], arrived.at[i]
        )
        for i in range(CHUNKS)
    ]
    numbers = pltpu.make_async_copy(ids_far, ids, arrived.at[CHUNKS])
    numbers.start()
    for copy in copies:
        copy.start()

    def clear(a, carry):
        rows = pl.ds(pl.multiple_of(a * width, width), width)
        dense[:, rows, :] = jnp.zeros((dense.shape[0], width, dense.shape[2]), bf16)
        return carry

    lax.fori_loop(0, cfg["rb"], clear, 0)
    numbers.wait()
    for i, copy in enumerate(copies):
        copy.wait()

        def step(j, carry, i=i):
            for u in range(GROUP):
                k = i * size + j * GROUP + u
                a = ids[k] // fb
                b = ids[k] - a * fb
                h = b // zb
                down = pl.ds(pl.multiple_of(a * width, width), width)
                across = pl.ds(pl.multiple_of((b - h * zb) * width, width), width)
                dense[h, down, across] = x[k]
            return carry

        lax.fori_loop(0, size // GROUP, step, 0)


def forward_kernel(cfg, group, x, *refs):
    parts, total = refs[: len(group)], refs[-1]
    rows = cfg["nb"] * cfg["width"]

    for i in range(cfg["cols"]):
        span = slice(i * rows, (i + 1) * rows)
        product = sum(
            jnp.dot(
                x[row_slot(cfg, g), span, :], part[: x.shape[2], :], preferred_element_type=f32
            )
            for g, part in zip(group, parts)
        )
        if len(refs) > len(group) + 1:
            product = refs[len(group)][span, :] + product
        total[span, :] = product


def forward_last_kernel(cfg, group, sent, x, *refs):
    parts = refs[: cfg["rows"]]
    total, out = refs[cfg["rows"] : cfg["rows"] + 2]
    rows = cfg["nb"] * cfg["width"]
    chips = cfg["cols"] // 2
    for i in range(chips):
        slot = column_slot(cfg, i, 1 if sent else 0)
        span = pl.ds(pl.multiple_of(slot * rows, rows), rows)
        value = total[span, :]
        for g in group:
            value = value + jnp.dot(
                x[row_slot(cfg, g), span, :], parts[g][: x.shape[2], :], preferred_element_type=f32
            )
        out[i * rows : (i + 1) * rows, :] = value.astype(out.dtype)
    if sent:
        tile = to_tail([from_tail(tree([tail_of(part) for part in parts]))])
        out[chips * rows :, :] = tile
        refs[-1][...] = tile


def merge_kernel(cfg, *refs):
    keep, keep_tail, received = refs[:3]
    own, own_tail, *sends = refs[3:]
    rows = cfg["nb"] * cfg["width"]
    tile = keep_tail[...].astype(f32) + tail_of(received)
    tile = to_tail([from_tail(tile)])
    own[...] = keep[:rows, :] + received[:rows, :].astype(f32)
    own_tail[...] = tile
    for k, send in enumerate(sends, start=1):
        span = slice(k * rows, (k + 1) * rows)
        send[:rows, :] = (keep[span, :] + received[span, :].astype(f32)).astype(bf16)
        send[rows:, :] = tile


def scale_kernel(cfg, first, *refs):
    chips = cfg["cols"] // 2
    own, own_tail = refs[:2]
    received = refs[2 : 1 + chips]
    rest = refs[1 + chips :]
    rows = own.shape[0]
    projected = tree([own[...]] + [r[:rows, :].astype(f32) for r in received])
    if first:
        removed, margins, direction, scaled, kept, spread = rest
        width = cfg["width"]
        for j in range(cfg["nb"]):
            logistic = 1.0 / (1.0 + jnp.exp(-margins[pl.ds(here()[0] * cfg["nb"] + j, 1), :]))
            weight = jnp.where(removed[j : j + 1, :] > 0.0, 0.0, logistic * (1.0 - logistic))
            row = jnp.broadcast_to(weight, (width, width))
            spread[j * width : (j + 1) * width, :] = row.T
        d = direction[...]
        norm = column_sum(d * d)
    else:
        spread, residual, old, before, norm_now, scaled, kept, direction, norm_out, beta_out = rest
        tile = tree([own_tail[...].astype(f32)] + [tail_of(r) for r in received])
        norm = from_tail(tile)
        beta = norm / norm_now[0:1, :]
        projected = projected + beta * before[...]
        d = residual[...] + beta * old[...]
        direction[...] = d
        norm_out[...] = jnp.broadcast_to(norm, norm_out.shape)
        beta_out[...] = jnp.broadcast_to(beta, beta_out.shape)
    kept[...] = projected
    weighted = spread[...] * projected
    width = cfg["width"]
    for j in range(cfg["nb"]):
        tile = weighted[j * width : (j + 1) * width, :]
        scaled[j * width : (j + 1) * width, :] = tile.T.astype(bf16)
    curvature = column_sum(weighted * projected) + RIDGE * column_sum(d * d)
    scaled[rows:, :] = to_tail([curvature, norm] if first else [curvature])


def turned(cfg, part):
    width = cfg["width"]
    return jnp.concatenate(
        [part[j * width : (j + 1) * width, :] for j in range(cfg["nb"])], axis=1
    )


def backward_sum(cfg, group, x, near, h):
    rows = cfg["nb"] * cfg["width"]
    products = []
    for g, part in zip(group, near):
        slot = column_slot(cfg, g // 2, g % 2)
        span = pl.ds(pl.multiple_of(slot * rows, rows), rows)
        products.append(jnp.dot(part, x[h, span, :], preferred_element_type=f32))
    return sum(products)


def backward_kernel(cfg, group, x, *refs):
    near = [turned(cfg, part) for part in refs[: len(group)]]
    total = refs[-1]
    for h in range(cfg["rows"]):
        product = backward_sum(cfg, group, x, near, h)
        if len(refs) > len(group) + 1:
            product = refs[len(group)][h] + product
        total[h] = product


def backward_last_kernel(cfg, group, first, sent, x, *refs):
    cols, width = cfg["cols"], cfg["width"]
    parts, total = refs[:cols], refs[cols]
    near = [turned(cfg, parts[g]) for g in group]
    outs = refs[cols + 1 :]
    if sent:
        tile = tree([tail_of(part) for part in parts])
        tile = to_tail([from_tail(tile, j) for j in range(2 if first else 1)])
        outs[-1][...] = tile
    for k in range(1, cfg["rows"]) if sent else [0]:
        out = outs[k - 1] if sent else outs[0]
        h = row_slot(cfg, k)
        value = total[h] + backward_sum(cfg, group, x, near, h)
        for j in range(cfg["zb"]):
            out[j * width : (j + 1) * width, :] = value[:, j * width : (j + 1) * width].astype(
                out.dtype
            )
        if sent:
            out[cfg["zb"] * width :, :] = tile


def update_kernel(cfg, first, *refs):
    others = cfg["rows"] - 1
    own, own_tail = refs[:2]
    received = refs[2 : 2 + others]
    direction, residual, norm_now, share, after, norm_out, alpha_out = refs[2 + others :]
    rows = own.shape[0]
    image = tree([own[...]] + [r[:rows, :].astype(f32) for r in received])
    width = cfg["width"]
    image = [image[j * width : (j + 1) * width, :].T for j in range(cfg["zb"])]
    image = jnp.concatenate(image, axis=0) + RIDGE * direction[...]
    tile = tree([own_tail[...].astype(f32)] + [tail_of(r) for r in received])
    norm = from_tail(tile, 1) if first else norm_now[0:1, :]
    alpha = norm / from_tail(tile)
    left = residual[...] - alpha * image
    after[...] = left
    norm_out[...] = jnp.broadcast_to(norm, norm_out.shape)
    alpha_out[...] = jnp.broadcast_to(alpha, alpha_out.shape)
    share[:rows, :] = left.astype(bf16)
    share[rows:, :] = to_tail([column_sum(left * left)])


def result_kernel(cfg, count, *refs):
    others = cfg["rows"]
    grads = refs[0]
    shares = refs[1 : 1 + others * (count - 1)]
    rest = refs[1 + len(shares) :]
    alphas, betas, out = rest[:count], rest[count : 2 * count - 1], rest[-1]
    rows = grads.shape[0] // others
    for k in range(others):
        span = pl.ds(pl.multiple_of(row_slot(cfg, k) * rows, rows), rows)
        d = grads[span, :]
        total = alphas[0][0:1, :] * d
        for j in range(1, count):
            share = shares[(j - 1) * others + k]
            d = share[:rows, :].astype(f32) + betas[j - 1][0:1, :] * d
            total = total + alphas[j][0:1, :] * d
        out[span, :] = total


def residual_kernel(cfg, *refs):
    shares, out = refs[:-1], refs[-1]
    rows = out.shape[0] // cfg["rows"]
    for k, share in enumerate(shares):
        span = pl.ds(pl.multiple_of(row_slot(cfg, k) * rows, rows), rows)
        out[span, :] = share[:rows, :].astype(f32)


def on_device(cfg, x_blocks, block_ids, margins, deleted, grads):
    width = x_blocks.shape[1]
    directions = grads.shape[1]
    cols, rows_axis = cfg["cols"], cfg["rows"]
    rb, fb = margins.shape[0] // width, grads.shape[0] // width
    nb, zb = rb // cols, fb // rows_axis
    cfg = dict(cfg, rb=rb, fb=fb, nb=nb, zb=zb, width=width)
    c, z = lax.axis_index("col"), lax.axis_index("row")
    ids = block_ids[:, 0]
    own_rows, own_features = nb * width, zb * width
    chips = cols // 2
    half = rb // 2 * width

    def shape(rows, dtype):
        return jax.ShapeDtypeStruct((rows, directions), dtype)

    def moved(value, to):
        pairs = [(r * cols + q, to(r, q)) for r in range(rows_axis) for q in range(cols)]
        return lax.ppermute(value, ("row", "col"), pairs)

    def across(value):
        return moved(value, lambda r, q: r * cols + (q ^ 1))

    def along_row(values):
        return [
            moved(
                values[i - 1],
                lambda r, q, i=i: (r ^ partner(row_partners(rows_axis), i, q & 1)) * cols + q,
            )
            for i in row_order(rows_axis)
        ]

    def along_col(values):
        return [
            moved(
                values[i - 1],
                lambda r, q, i=i: r * cols + (q ^ (2 * partner(range(chips), i, q & 1))),
            )
            for i in chip_order(chips)
        ]

    def near(value):
        return pltpu.with_memory_space_constraint(value, pltpu.VMEM)

    def far(value):
        return pltpu.with_memory_space_constraint(value, pltpu.HBM)

    def call(kernel, out, inputs, stay=True, aliases=None):
        if stay:
            out = [pltpu.VMEM(o.shape, o.dtype) for o in out]
        return pl.pallas_call(
            kernel,
            out_shape=out,
            in_specs=[VMEM] * len(inputs),
            out_specs=[VMEM] * len(out),
            input_output_aliases=aliases or {},
            compiler_params=pltpu.CompilerParams(vmem_limit_bytes=4 << 20),
        )(*map(near, inputs))

    matrix = []

    def multiply(kernel, out, inputs, aliases=None):
        at = len(inputs)

        def body(*refs):
            kernel(refs[at], *refs[:at], *refs[at + 1 : -1])

        x = matrix.pop()
        *results, x = call(
            body,
            [*out, jax.ShapeDtypeStruct(x.shape, x.dtype)],
            [*inputs, x],
            aliases={**(aliases or {}), at: len(out)},
        )
        matrix.append(x)
        return results

    def begin():
        return pl.pallas_call(
            functools.partial(first_kernel, cfg),
            out_shape=[
                pltpu.VMEM((half + TAIL, directions), bf16),
                pltpu.VMEM((half, directions), f32),
                pltpu.VMEM((TAIL, directions), bf16),
                pltpu.VMEM((own_features, directions), f32),
            ],
            in_specs=[pl.BlockSpec(memory_space=pltpu.HBM)] * 3,
            out_specs=[VMEM] * 4,
            scratch_shapes=[
                pltpu.SMEM(ids.shape, jnp.int32),
                pltpu.SMEM((cols,), jnp.int32),
                pltpu.VMEM(x_blocks.shape, bf16),
                pltpu.VMEM(grads.shape, f32),
                pltpu.VMEM((fb, width, directions), bf16),
                pltpu.VMEM((rb, width, directions), f32),
                pltpu.SemaphoreType.DMA((CHUNKS + 2,)),
            ],
            compiler_params=pltpu.CompilerParams(vmem_limit_bytes=16 << 20),
        )(far(ids), far(x_blocks), far(grads))

    def lay_out():
        return pl.pallas_call(
            functools.partial(dense_kernel, cfg),
            out_shape=pltpu.VMEM((rows_axis, rb * width, own_features), bf16),
            in_specs=[pl.BlockSpec(memory_space=pltpu.HBM)] * 2,
            out_specs=VMEM,
            scratch_shapes=[
                pltpu.SMEM(ids.shape, jnp.int32),
                pltpu.VMEM(x_blocks.shape, bf16),
                pltpu.SemaphoreType.DMA((CHUNKS + 1,)),
            ],
            compiler_params=pltpu.CompilerParams(vmem_limit_bytes=12 << 20),
        )(far(ids), far(x_blocks))

    def forward(parts):
        total = []
        *groups, group = row_groups(rows_axis)
        for some in groups:
            total = multiply(
                functools.partial(forward_kernel, cfg, some),
                [shape(rb * width, f32)],
                [parts[g] for g in some] + total,
                aliases={len(some): 0} if total else {},
            )
        send, keep_tail = multiply(
            functools.partial(forward_last_kernel, cfg, group, True),
            [shape(half + TAIL, bf16), shape(TAIL, bf16)],
            [*parts, *total],
        )
        (keep,) = multiply(
            functools.partial(forward_last_kernel, cfg, group, False),
            [shape(half, f32)],
            [*parts, *total],
        )
        return send, keep, keep_tail

    def backward(scaled, first):
        others = along_col([scaled] * (chips - 1))
        parts = []
        for part in [scaled, *others]:
            parts += [part, across(part)]
        total = []
        *groups, group = column_groups(chips)
        for some in groups:
            total = multiply(
                functools.partial(backward_kernel, cfg, some),
                [jax.ShapeDtypeStruct((rows_axis, directions, own_features), f32)],
                [parts[g] for g in some] + total,
                aliases={len(some): 0} if total else {},
            )
        *sends, own_tail = multiply(
            functools.partial(backward_last_kernel, cfg, group, first, True),
            [shape(own_features + TAIL, bf16)] * (rows_axis - 1) + [shape(TAIL, bf16)],
            [*parts, *total],
        )
        (own,) = multiply(
            functools.partial(backward_last_kernel, cfg, group, first, False),
            [shape(own_features, f32)],
            [*parts, *total],
        )
        return sends, own, own_tail

    row_ids = z * margins.shape[0] + c * own_rows + jnp.arange(own_rows, dtype=jnp.int32)
    row_ids = row_ids.reshape(nb, width)
    removed = jnp.any(row_ids[None] == deleted[:, None, None], axis=0).astype(f32)
    margins = margins.reshape(rb, width)
    parts, shares, alphas, betas = [], [], [], []
    share = spread = before = None
    norm_now = jnp.zeros((8, directions), f32)
    for iteration in range(ITERS):
        first = iteration == 0
        if first:
            send, keep, keep_tail, direction = begin()
            residual = direction
        else:
            parts = [share, *along_row([share] * (rows_axis - 1))]
            shares += parts
            send, keep, keep_tail = forward(parts)
        received = across(send)
        own, own_tail, *sends = call(
            functools.partial(merge_kernel, cfg),
            [shape(own_rows, f32), shape(TAIL, bf16)]
            + [shape(own_rows + TAIL, bf16)] * (chips - 1),
            [keep, keep_tail, received],
        )
        received = along_col(sends)
        if first:
            matrix.append(lay_out())
            scaled, before, spread = call(
                functools.partial(scale_kernel, cfg, True),
                [shape(own_rows + TAIL, bf16), shape(own_rows, f32), shape(own_rows, f32)],
                [own, own_tail, *received, removed, margins, direction],
            )
        else:
            scaled, before, direction, norm_now, beta = call(
                functools.partial(scale_kernel, cfg, False),
                [
                    shape(own_rows + TAIL, bf16),
                    shape(own_rows, f32),
                    shape(own_features, f32),
                    shape(8, f32),
                    shape(8, f32),
                ],
                [own, own_tail, *received, spread, residual, direction, before, norm_now],
            )
            betas.append(beta)
        sends, own, own_tail = backward(scaled, first)
        received = along_row(sends)
        share, residual, norm_now, alpha = call(
            functools.partial(update_kernel, cfg, first),
            [
                shape(own_features + TAIL, bf16),
                shape(own_features, f32),
                shape(8, f32),
                shape(8, f32),
            ],
            [own, own_tail, *received, direction, residual, norm_now],
        )
        alphas.append(alpha)
    parts = [share, *along_row([share] * (rows_axis - 1))]
    (answer,) = call(
        functools.partial(result_kernel, cfg, ITERS),
        [shape(fb * width, f32)],
        [grads, *shares, *alphas, *betas],
        stay=False,
    )
    (left,) = call(
        functools.partial(residual_kernel, cfg), [shape(fb * width, f32)], parts, stay=False
    )
    return (answer, left)


def solution(mesh):
    cfg = {"rows": mesh.shape["row"], "cols": mesh.shape["col"]}
    placed = (P("row", "col", None), P("row", "col"), P("row"), P("row"), P("col", None))
    return jax.shard_map(
        functools.partial(on_device, cfg),
        mesh=mesh,
        in_specs=placed,
        out_specs=(P("col", None), P("col", None)),
        check_vma=False,
    )
```

```python
import functools

import jax
import jax.numpy as jnp
from jax import lax
from jax.experimental import pallas as pl
from jax.experimental.pallas import tpu as pltpu
from jax.sharding import PartitionSpec as P


ITERS = 3
RIDGE = 0.2
TAIL = 8

GROUP = 32
CHUNKS = 8


def crossed(k, n):
    return (k & ~3) | ((k & 1) << 1) | ((k >> 1) & 1) if n > 2 else k


def row_partners(n):
    basis = [n - 1, *(1 << b for b in range(n.bit_length() - 2))]
    order = [0]
    for value in basis:
        order += [k ^ value for k in order]
    return order


def partner(order, i, odd):
    k = order[i]
    return k + odd * (crossed(k, len(order)) - k)


def row_order(n):
    return list(range(1, n))


def row_groups(n):
    return [*([k] for k in range(n - 2)), [n - 2, n - 1]]


def chip_order(n):
    return list(range(1, n))


def column_groups(n):
    order = chip_order(n)
    between = [[2 * before + 1, 2 * k] for before, k in zip(order, order[1:])]
    return [[0], [1, 2 * order[0]], *between, [2 * order[-1] + 1]]


f32 = jnp.float32
bf16 = jnp.bfloat16
VMEM = pl.BlockSpec(memory_space=pltpu.VMEM)


def tree(values):
    while len(values) > 1:
        values = [values[i] + values[i + 1] for i in range(0, len(values), 2)]
    return values[0]


def to_tail(sums):
    rows = lax.broadcasted_iota(jnp.int32, (TAIL, sums[0].shape[1]), 0)
    tile = jnp.zeros(rows.shape, f32)
    for position, value in enumerate(sums):
        for part in range(3):
            piece = value.astype(bf16).astype(f32)
            tile = jnp.where(rows == 3 * position + part, piece, tile)
            value = value - piece
    return tile.astype(bf16)


def from_tail(tile, position=0):
    start = 3 * position
    return tile[start : start + 1] + tile[start + 1 : start + 2] + tile[start + 2 : start + 3]


def tail_of(ref):
    rows = ref.shape[0]
    return ref[rows - TAIL : rows, :].astype(f32)


def column_sum(value):
    return jnp.sum(value, axis=0, keepdims=True)


def here():
    return lax.axis_index("col"), lax.axis_index("row")


def row_slot(cfg, i):
    c, z = here()
    return z ^ partner(row_partners(cfg["rows"]), i, c & 1)


def column_slot(cfg, i, across):
    c = here()[0] ^ across
    return c ^ (2 * partner(range(cfg["cols"] // 2), i, c & 1))


def first_kernel(
    cfg,
    ids_far,
    listed,
    far,
    send,
    keep,
    keep_tail,
    direction,
    ids,
    places,
    x,
    near,
    held,
    total,
    arrived,
):
    fb, nb = cfg["fb"], cfg["nb"]
    chips = cfg["cols"] // 2
    for across in range(2):
        for i in range(chips):
            places[column_slot(cfg, i, across)] = across * chips + i
    z = here()[1]
    count = ids.shape[0]
    size = count // CHUNKS
    numbers = pltpu.make_async_copy(ids_far, ids, arrived.at[CHUNKS + 1])
    head = pltpu.make_async_copy(far, near, arrived.at[CHUNKS])
    numbers.start()
    head.start()
    copies = [
        pltpu.make_async_copy(
            listed.at[pl.ds(i * size, size)], x.at[pl.ds(i * size, size)], arrived.at[i]
        )
        for i in range(CHUNKS)
    ]
    for copy in copies:
        copy.start()
    total[...] = jnp.zeros_like(total)
    numbers.wait()
    head.wait()
    own = direction.shape[0]
    direction[...] = near[pl.ds(pl.multiple_of(z * own, own), own), :]
    held[...] = near[...].astype(bf16).reshape(held.shape)
    for i, copy in enumerate(copies):
        copy.wait()

        def step(j, carry, i=i):
            products = []
            for u in range(GROUP):
                k = i * size + j * GROUP + u
                a = ids[k] // fb
                b = ids[k] - a * fb
                slot = a // nb
                target = places[slot] * nb + (a - slot * nb)
                products.append((target, jnp.dot(x[k], held[b], preferred_element_type=f32)))
            for target, product in products:
                total[target] = total[target] + product
            return carry

        lax.fori_loop(0, size // GROUP, step, 0)
    half = total.shape[0] // 2
    rows = keep.shape[0]
    keep[...] = total[:half].reshape(keep.shape)
    send[:rows, :] = total[half:].reshape(keep.shape).astype(bf16)
    send[rows:, :] = jnp.zeros((TAIL, send.shape[1]), bf16)
    keep_tail[...] = jnp.zeros(keep_tail.shape, bf16)


def dense_kernel(cfg, ids_far, listed, dense, ids, x, arrived):
    fb, zb, width = cfg["fb"], cfg["zb"], cfg["width"]
    size = x.shape[0] // CHUNKS
    copies = [
        pltpu.make_async_copy(
            listed.at[pl.ds(i * size, size)], x.at[pl.ds(i * size, size)], arrived.at[i]
        )
        for i in range(CHUNKS)
    ]
    numbers = pltpu.make_async_copy(ids_far, ids, arrived.at[CHUNKS])
    numbers.start()
    for copy in copies:
        copy.start()

    def clear(a, carry):
        rows = pl.ds(pl.multiple_of(a * width, width), width)
        dense[:, rows, :] = jnp.zeros((dense.shape[0], width, dense.shape[2]), bf16)
        return carry

    lax.fori_loop(0, cfg["rb"], clear, 0)
    numbers.wait()
    for i, copy in enumerate(copies):
        copy.wait()

        def step(j, carry, i=i):
            for u in range(GROUP):
                k = i * size + j * GROUP + u
                a = ids[k] // fb
                b = ids[k] - a * fb
                h = b // zb
                down = pl.ds(pl.multiple_of(a * width, width), width)
                across = pl.ds(pl.multiple_of((b - h * zb) * width, width), width)
                dense[h, down, across] = x[k]
            return carry

        lax.fori_loop(0, size // GROUP, step, 0)


def forward_kernel(cfg, group, x, *refs):
    parts, total = refs[: len(group)], refs[-1]
    rows = cfg["nb"] * cfg["width"]

    for i in range(cfg["cols"]):
        span = slice(i * rows, (i + 1) * rows)
        product = sum(
            jnp.dot(
                x[row_slot(cfg, g), span, :], part[: x.shape[2], :], preferred_element_type=f32
            )
            for g, part in zip(group, parts)
        )
        if len(refs) > len(group) + 1:
            product = refs[len(group)][span, :] + product
        total[span, :] = product


def forward_last_kernel(cfg, group, sent, x, *refs):
    parts = refs[: cfg["rows"]]
    total, out = refs[cfg["rows"] : cfg["rows"] + 2]
    rows = cfg["nb"] * cfg["width"]
    chips = cfg["cols"] // 2
    for i in range(chips):
        slot = column_slot(cfg, i, 1 if sent else 0)
        span = pl.ds(pl.multiple_of(slot * rows, rows), rows)
        value = total[span, :]
        for g in group:
            value = value + jnp.dot(
                x[row_slot(cfg, g), span, :], parts[g][: x.shape[2], :], preferred_element_type=f32
            )
        out[i * rows : (i + 1) * rows, :] = value.astype(out.dtype)
    if sent:
        tile = to_tail([from_tail(tree([tail_of(part) for part in parts]))])
        out[chips * rows :, :] = tile
        refs[-1][...] = tile


def merge_kernel(cfg, *refs):
    keep, keep_tail, received = refs[:3]
    own, own_tail, *sends = refs[3:]
    rows = cfg["nb"] * cfg["width"]
    tile = keep_tail[...].astype(f32) + tail_of(received)
    tile = to_tail([from_tail(tile)])
    own[...] = keep[:rows, :] + received[:rows, :].astype(f32)
    own_tail[...] = tile
    for k, send in enumerate(sends, start=1):
        span = slice(k * rows, (k + 1) * rows)
        send[:rows, :] = (keep[span, :] + received[span, :].astype(f32)).astype(bf16)
        send[rows:, :] = tile


def scale_kernel(cfg, first, last, *refs):
    chips = cfg["cols"] // 2
    own, own_tail = refs[:2]
    received = refs[2 : 1 + chips]
    rest = refs[1 + chips :]
    rows = own.shape[0]
    projected = tree([own[...]] + [r[:rows, :].astype(f32) for r in received])
    if first:
        removed, margins, direction, scaled, spread = rest[:5]
        width = cfg["width"]
        for j in range(cfg["nb"]):
            logistic = 1.0 / (1.0 + jnp.exp(-margins[pl.ds(here()[0] * cfg["nb"] + j, 1), :]))
            weight = jnp.where(removed[j : j + 1, :] > 0.0, 0.0, logistic * (1.0 - logistic))
            row = jnp.broadcast_to(weight, (width, width))
            spread[j * width : (j + 1) * width, :] = row.T
        d = direction[...]
        norm = column_sum(d * d)
    else:
        spread, residual, old, before, norm_now, scaled, direction, norm_out, beta_out = rest[:9]
        tile = tree([own_tail[...].astype(f32)] + [tail_of(r) for r in received])
        norm = from_tail(tile)
        beta = norm / norm_now[0:1, :]
        projected = projected + beta * before[...]
        d = residual[...] + beta * old[...]
        direction[...] = d
        norm_out[...] = jnp.broadcast_to(norm, norm_out.shape)
        beta_out[...] = jnp.broadcast_to(beta, beta_out.shape)
    if not last:
        rest[-1][...] = projected
    weighted = spread[...] * projected
    width = cfg["width"]
    for j in range(cfg["nb"]):
        tile = weighted[j * width : (j + 1) * width, :]
        scaled[j * width : (j + 1) * width, :] = tile.T.astype(bf16)
    curvature = column_sum(weighted * projected) + RIDGE * column_sum(d * d)
    scaled[rows:, :] = to_tail([curvature, norm] if first else [curvature])


def turned(cfg, part):
    width = cfg["width"]
    return jnp.concatenate(
        [part[j * width : (j + 1) * width, :] for j in range(cfg["nb"])], axis=1
    )


def backward_sum(cfg, group, x, near, h):
    rows = cfg["nb"] * cfg["width"]
    products = []
    for g, part in zip(group, near):
        slot = column_slot(cfg, g // 2, g % 2)
        span = pl.ds(pl.multiple_of(slot * rows, rows), rows)
        products.append(jnp.dot(part, x[h, span, :], preferred_element_type=f32))
    return sum(products)


def backward_kernel(cfg, group, x, *refs):
    near = [turned(cfg, part) for part in refs[: len(group)]]
    total = refs[-1]
    for h in range(cfg["rows"]):
        product = backward_sum(cfg, group, x, near, h)
        if len(refs) > len(group) + 1:
            product = refs[len(group)][h] + product
        total[h] = product


def backward_last_kernel(cfg, group, first, sent, x, *refs):
    cols, width = cfg["cols"], cfg["width"]
    parts, total = refs[:cols], refs[cols]
    near = [turned(cfg, parts[g]) for g in group]
    outs = refs[cols + 1 :]
    if sent:
        tile = tree([tail_of(part) for part in parts])
        tile = to_tail([from_tail(tile, j) for j in range(2 if first else 1)])
        outs[-1][...] = tile
    for k in range(1, cfg["rows"]) if sent else [0]:
        out = outs[k - 1] if sent else outs[0]
        h = row_slot(cfg, k)
        value = total[h] + backward_sum(cfg, group, x, near, h)
        for j in range(cfg["zb"]):
            out[j * width : (j + 1) * width, :] = value[:, j * width : (j + 1) * width].astype(
                out.dtype
            )
        if sent:
            out[cfg["zb"] * width :, :] = tile


def update_kernel(cfg, first, *refs):
    others = cfg["rows"] - 1
    own, own_tail = refs[:2]
    received = refs[2 : 2 + others]
    direction, residual, norm_now, share, alpha_out, *kept = refs[2 + others :]
    rows = own.shape[0]
    image = tree([own[...]] + [r[:rows, :].astype(f32) for r in received])
    width = cfg["width"]
    image = [image[j * width : (j + 1) * width, :].T for j in range(cfg["zb"])]
    image = jnp.concatenate(image, axis=0) + RIDGE * direction[...]
    tile = tree([own_tail[...].astype(f32)] + [tail_of(r) for r in received])
    norm = from_tail(tile, 1) if first else norm_now[0:1, :]
    alpha = norm / from_tail(tile)
    left = residual[...] - alpha * image
    if kept:
        kept[0][...] = left
        kept[1][...] = jnp.broadcast_to(norm, kept[1].shape)
    alpha_out[...] = jnp.broadcast_to(alpha, alpha_out.shape)
    share[:rows, :] = left.astype(bf16)
    share[rows:, :] = to_tail([column_sum(left * left)])


def result_kernel(cfg, count, *refs):
    others = cfg["rows"]
    grads = refs[0]
    shares = refs[1 : 1 + others * (count - 1)]
    rest = refs[1 + len(shares) :]
    alphas, betas, out = rest[:count], rest[count : 2 * count - 1], rest[-1]
    rows = grads.shape[0] // others
    for k in range(others):
        span = pl.ds(pl.multiple_of(row_slot(cfg, k) * rows, rows), rows)
        d = grads[span, :]
        total = alphas[0][0:1, :] * d
        for j in range(1, count):
            share = shares[(j - 1) * others + k]
            d = share[:rows, :].astype(f32) + betas[j - 1][0:1, :] * d
            total = total + alphas[j][0:1, :] * d
        out[span, :] = total


def residual_kernel(cfg, *refs):
    shares, out = refs[:-1], refs[-1]
    rows = out.shape[0] // cfg["rows"]
    for k, share in enumerate(shares):
        span = pl.ds(pl.multiple_of(row_slot(cfg, k) * rows, rows), rows)
        out[span, :] = share[:rows, :].astype(f32)


def on_device(cfg, x_blocks, block_ids, margins, deleted, grads):
    width = x_blocks.shape[1]
    directions = grads.shape[1]
    cols, rows_axis = cfg["cols"], cfg["rows"]
    rb, fb = margins.shape[0] // width, grads.shape[0] // width
    nb, zb = rb // cols, fb // rows_axis
    cfg = dict(cfg, rb=rb, fb=fb, nb=nb, zb=zb, width=width)
    c, z = lax.axis_index("col"), lax.axis_index("row")
    ids = block_ids[:, 0]
    own_rows, own_features = nb * width, zb * width
    chips = cols // 2
    half = rb // 2 * width

    def shape(rows, dtype):
        return jax.ShapeDtypeStruct((rows, directions), dtype)

    def moved(value, to):
        pairs = [(r * cols + q, to(r, q)) for r in range(rows_axis) for q in range(cols)]
        return lax.ppermute(value, ("row", "col"), pairs)

    def across(value):
        return moved(value, lambda r, q: r * cols + (q ^ 1))

    def along_row(values):
        return [
            moved(
                values[i - 1],
                lambda r, q, i=i: (r ^ partner(row_partners(rows_axis), i, q & 1)) * cols + q,
            )
            for i in row_order(rows_axis)
        ]

    def along_col(values):
        return [
            moved(
                values[i - 1],
                lambda r, q, i=i: r * cols + (q ^ (2 * partner(range(chips), i, q & 1))),
            )
            for i in chip_order(chips)
        ]

    def near(value):
        return pltpu.with_memory_space_constraint(value, pltpu.VMEM)

    def far(value):
        return pltpu.with_memory_space_constraint(value, pltpu.HBM)

    def call(kernel, out, inputs, stay=True, aliases=None):
        if stay:
            out = [pltpu.VMEM(o.shape, o.dtype) for o in out]
        return pl.pallas_call(
            kernel,
            out_shape=out,
            in_specs=[VMEM] * len(inputs),
            out_specs=[VMEM] * len(out),
            input_output_aliases=aliases or {},
            compiler_params=pltpu.CompilerParams(vmem_limit_bytes=4 << 20),
        )(*map(near, inputs))

    matrix = []

    def multiply(kernel, out, inputs, aliases=None):
        at = len(inputs)

        def body(*refs):
            kernel(refs[at], *refs[:at], *refs[at + 1 : -1])

        x = matrix.pop()
        *results, x = call(
            body,
            [*out, jax.ShapeDtypeStruct(x.shape, x.dtype)],
            [*inputs, x],
            aliases={**(aliases or {}), at: len(out)},
        )
        matrix.append(x)
        return results

    def begin():
        return pl.pallas_call(
            functools.partial(first_kernel, cfg),
            out_shape=[
                pltpu.VMEM((half + TAIL, directions), bf16),
                pltpu.VMEM((half, directions), f32),
                pltpu.VMEM((TAIL, directions), bf16),
                pltpu.VMEM((own_features, directions), f32),
            ],
            in_specs=[pl.BlockSpec(memory_space=pltpu.HBM)] * 3,
            out_specs=[VMEM] * 4,
            scratch_shapes=[
                pltpu.SMEM(ids.shape, jnp.int32),
                pltpu.SMEM((cols,), jnp.int32),
                pltpu.VMEM(x_blocks.shape, bf16),
                pltpu.VMEM(grads.shape, f32),
                pltpu.VMEM((fb, width, directions), bf16),
                pltpu.VMEM((rb, width, directions), f32),
                pltpu.SemaphoreType.DMA((CHUNKS + 2,)),
            ],
            compiler_params=pltpu.CompilerParams(vmem_limit_bytes=16 << 20),
        )(far(ids), far(x_blocks), far(grads))

    def lay_out():
        return pl.pallas_call(
            functools.partial(dense_kernel, cfg),
            out_shape=pltpu.VMEM((rows_axis, rb * width, own_features), bf16),
            in_specs=[pl.BlockSpec(memory_space=pltpu.HBM)] * 2,
            out_specs=VMEM,
            scratch_shapes=[
                pltpu.SMEM(ids.shape, jnp.int32),
                pltpu.VMEM(x_blocks.shape, bf16),
                pltpu.SemaphoreType.DMA((CHUNKS + 1,)),
            ],
            compiler_params=pltpu.CompilerParams(vmem_limit_bytes=12 << 20),
        )(far(ids), far(x_blocks))

    def forward(parts):
        total = []
        *groups, group = row_groups(rows_axis)
        for some in groups:
            total = multiply(
                functools.partial(forward_kernel, cfg, some),
                [shape(rb * width, f32)],
                [parts[g] for g in some] + total,
                aliases={len(some): 0} if total else {},
            )
        send, keep_tail = multiply(
            functools.partial(forward_last_kernel, cfg, group, True),
            [shape(half + TAIL, bf16), shape(TAIL, bf16)],
            [*parts, *total],
        )
        (keep,) = multiply(
            functools.partial(forward_last_kernel, cfg, group, False),
            [shape(half, f32)],
            [*parts, *total],
        )
        return send, keep, keep_tail

    def backward(scaled, first):
        others = along_col([scaled] * (chips - 1))
        parts = []
        for part in [scaled, *others]:
            parts += [part, across(part)]
        total = []
        *groups, group = column_groups(chips)
        for some in groups:
            total = multiply(
                functools.partial(backward_kernel, cfg, some),
                [jax.ShapeDtypeStruct((rows_axis, directions, own_features), f32)],
                [parts[g] for g in some] + total,
                aliases={len(some): 0} if total else {},
            )
        *sends, own_tail = multiply(
            functools.partial(backward_last_kernel, cfg, group, first, True),
            [shape(own_features + TAIL, bf16)] * (rows_axis - 1) + [shape(TAIL, bf16)],
            [*parts, *total],
        )
        (own,) = multiply(
            functools.partial(backward_last_kernel, cfg, group, first, False),
            [shape(own_features, f32)],
            [*parts, *total],
        )
        return sends, own, own_tail

    row_ids = z * margins.shape[0] + c * own_rows + jnp.arange(own_rows, dtype=jnp.int32)
    row_ids = row_ids.reshape(nb, width)
    removed = jnp.any(row_ids[None] == deleted[:, None, None], axis=0).astype(f32)
    margins = margins.reshape(rb, width)
    parts, shares, alphas, betas = [], [], [], []
    share = spread = before = None
    norm_now = jnp.zeros((8, directions), f32)
    for iteration in range(ITERS):
        first, last = iteration == 0, iteration == ITERS - 1
        if first:
            send, keep, keep_tail, direction = begin()
            residual = direction
        else:
            parts = [share, *along_row([share] * (rows_axis - 1))]
            shares += parts
            send, keep, keep_tail = forward(parts)
        received = across(send)
        own, own_tail, *sends = call(
            functools.partial(merge_kernel, cfg),
            [shape(own_rows, f32), shape(TAIL, bf16)]
            + [shape(own_rows + TAIL, bf16)] * (chips - 1),
            [keep, keep_tail, received],
        )
        received = along_col(sends)
        if first:
            matrix.append(lay_out())
            scaled, spread, before = call(
                functools.partial(scale_kernel, cfg, True, False),
                [shape(own_rows + TAIL, bf16), shape(own_rows, f32), shape(own_rows, f32)],
                [own, own_tail, *received, removed, margins, direction],
            )
        else:
            scaled, direction, norm_now, beta, *kept = call(
                functools.partial(scale_kernel, cfg, False, last),
                [
                    shape(own_rows + TAIL, bf16),
                    shape(own_features, f32),
                    shape(8, f32),
                    shape(8, f32),
                ]
                + [shape(own_rows, f32)] * (not last),
                [own, own_tail, *received, spread, residual, direction, before, norm_now],
            )
            before = None if last else kept[0]
            betas.append(beta)
        sends, own, own_tail = backward(scaled, first)
        received = along_row(sends)
        share, alpha, *kept = call(
            functools.partial(update_kernel, cfg, first),
            [shape(own_features + TAIL, bf16), shape(8, f32)]
            + [shape(own_features, f32), shape(8, f32)] * (not last),
            [own, own_tail, *received, direction, residual, norm_now],
        )
        residual, norm_now = (None, None) if last else kept
        alphas.append(alpha)
    parts = [share, *along_row([share] * (rows_axis - 1))]
    (answer,) = call(
        functools.partial(result_kernel, cfg, ITERS),
        [shape(fb * width, f32)],
        [grads, *shares, *alphas, *betas],
        stay=False,
    )
    (left,) = call(
        functools.partial(residual_kernel, cfg), [shape(fb * width, f32)], parts, stay=False
    )
    return (answer, left)


def solution(mesh):
    cfg = {"rows": mesh.shape["row"], "cols": mesh.shape["col"]}
    placed = (P("row", "col", None), P("row", "col"), P("row"), P("row"), P("col", None))
    return jax.shard_map(
        functools.partial(on_device, cfg),
        mesh=mesh,
        in_specs=placed,
        out_specs=(P("col", None), P("col", None)),
        check_vma=False,
    )
```
